256 devices in a mesh: group: 16 (over z, core), tok: 4 (over y), head: 4 (over x).
Axes of the slice: x: 4, y: 4, z: 8, core: 2. Of those that a mesh axis runs over, the one named last changes fastest.
Arguments:
- streams: bfloat16 [2, 32768, 2240], P(None, ('group', 'tok'), 'head'), may hold values from -6 to 6
- w_query: bfloat16 [2240, 2240], P(None, 'head'), may hold values from -0.125 to 0.125
- w_key: bfloat16 [2240, 2240], P(None, 'head'), may hold values from -0.125 to 0.125
- w_value: bfloat16 [2240, 2240], P(None, 'head'), may hold values from -0.125 to 0.125
- gain: float32 [2240], P('head'), may hold values from 0.25 to 1.75
Outputs:
- attended: bfloat16 [2, 32768, 2240], P(None, ('group', 'tok'), 'head')
The draws below stay inside these ranges and needn't reach their ends.
All inputs are finite; a program needn't handle non-finite values.
Results may differ from the reference program's by a relative error of at most 0.0053.
Values may be sent and summed in bfloat16 or wider, within the bound.
A program may use at most 64 MiB of HBM per device.

```python
import jax
import jax.numpy as jnp
from jax import lax

D = 2240
HEADS = 20
HEAD_DIM = 112
TOK_DEV = 512
TOKENS = 32768
N_GROUP = 16
N_TOK = 4


def block_levels(stream_key, extent, shards, least, largest):
    level = 1.0
    for position, blocks in shards:
        heights = jax.random.uniform(jax.random.fold_in(jax.random.fold_in(stream_key, 6), position), (blocks,), jnp.float32, least / len(shards), largest / len(shards))
        level = level * jnp.repeat(jnp.exp(heights), extent[position] // blocks).reshape((-1,) + (1,) * (len(extent) - 1 - position))
    return level


def normal_values(rng, shape, width, limit, split=(), kind=jnp.bfloat16):
    entries = width * jax.random.normal(rng, shape, jnp.float32)
    if split:
        entries = entries * block_levels(rng, shape, split, -0.22, 0.18)
    return jnp.clip(entries, -limit, limit).astype(kind)


def setup_inputs(seed: int = 0) -> dict:
    splits = jax.random.split(jax.random.key(seed), 6)
    return {
        "streams": normal_values(splits[0], (2, TOKENS, D), 1.0, 6.0, ((1, 64), (2, 4))),
        "w_query": normal_values(splits[1], (D, D), D ** -0.5, 0.125, ((1, 4),)),
        "w_key": normal_values(splits[2], (D, D), D ** -0.5, 0.125, ((1, 4),)),
        "w_value": normal_values(splits[3], (D, D), D ** -0.5, 0.125, ((1, 4),)),
        "gain": jnp.clip(1.0 + 0.15 * jax.random.normal(splits[4], (D,), jnp.float32), 0.25, 1.75),
    }


def project(block, matrix):
    return jnp.dot(block, matrix, preferred_element_type=jnp.float32).astype(jnp.bfloat16)

def group_state(key_rows, value_rows):
    key_heads = jnp.maximum(key_rows, 0).astype(jnp.float32).reshape(-1, HEADS, HEAD_DIM)
    value_heads = value_rows.astype(jnp.float32).reshape(-1, HEADS, HEAD_DIM)
    return jnp.einsum('tha,thb->hab', key_heads, value_heads, precision=lax.Precision.HIGHEST)

def read_norm(query_rows, totals, gain):
    query_heads = jnp.maximum(query_rows, 0).astype(jnp.float32).reshape(-1, HEADS, HEAD_DIM)
    reading = jnp.einsum('tha,hab->thb', query_heads, totals, precision=lax.Precision.HIGHEST)
    scale = lax.rsqrt(lax.optimization_barrier(jnp.mean(reading * reading, axis=-1, keepdims=True)) + 1e-06)
    normed = reading * scale * gain.reshape(HEADS, HEAD_DIM)
    return normed.reshape(-1, D).astype(jnp.bfloat16)

def reference(streams, w_query, w_key, w_value, gain):
    group_len = TOK_DEV * N_TOK
    clean_blocks = streams[0].reshape(N_GROUP, group_len, D)
    noisy_blocks = streams[1].reshape(N_GROUP, group_len, D)

    def step(prefix, blocks):
        clean, noisy = blocks
        clean_state = group_state(project(clean, w_key), project(clean, w_value))
        noisy_state = group_state(project(noisy, w_key), project(noisy, w_value))
        clean_out = read_norm(project(clean, w_query), prefix + clean_state, gain)
        noisy_out = read_norm(project(noisy, w_query), prefix + noisy_state, gain)
        return (prefix + clean_state, (clean_out, noisy_out))
    start = jnp.zeros((HEADS, HEAD_DIM, HEAD_DIM), jnp.float32)
    final, outputs = lax.scan(step, start, (clean_blocks, noisy_blocks))
    clean_all = outputs[0].reshape(N_GROUP * group_len, D)
    noisy_all = outputs[1].reshape(N_GROUP * group_len, D)
    return jnp.stack([clean_all, noisy_all], axis=0)
```

```python
import functools

import jax
import jax.numpy as jnp
from jax import lax
from jax.experimental import pallas as pl
from jax.experimental.pallas import tpu as pltpu
from jax.sharding import PartitionSpec as P

MESH = pl.DeviceIdType.MESH
F32 = jnp.float32
BF16 = jnp.bfloat16

HD = 112
LN = 128
NH = 5
NX = 4
NY = 4
NZ = 8
DW = 560
MAIN = 512
TAIL = 48
TOK = 512
ROWS = 2 * TOK
CH = 128
NC = ROWS // CH
KW = NX * MAIN + NX * 64
PW = NH * LN
QR = PW // NY
ER = QR // 2


def rcopy(src, dst, ssem, rsem, where):
    return pltpu.make_async_remote_copy(
        src_ref=src, dst_ref=dst, send_sem=ssem, recv_sem=rsem, device_id=where, device_id_type=MESH
    )


def kernel(
    streams, wq, wk, wv, gain, out,
    raw, wcat, stage, xbuf, tbuf, qkv, obuf, st32, st16, rsbuf, cst, csend, crecv,
    zsend, zrecv, psend, precv, pfx, tot,
    lsem, wsem, osem, xs, xr, fs, fr, ts, tr, us, ur, ys, yr, cs, cr, zs, zr,
):
    x = lax.axis_index("head")
    y = lax.axis_index("tok")
    g = lax.axis_index("group")
    z, core = g // 2, g % 2
    right, left = (x + 1) % NX, (x + NX - 1) % NX
    mate = g + 1 - 2 * core
    side = (right, left)

    barrier = pltpu.get_barrier_semaphore()
    partners = [{"head": right}, {"head": left}, {"group": mate}]
    partners += [{"tok": (y + d) % NY} for d in range(1, NY)]
    partners += [{"group": ((z + d) % NZ) * 2 + core} for d in range(1, NZ)]
    for where in partners:
        pl.semaphore_signal(barrier, inc=1, device_id=where, device_id_type=MESH)

    stage_copy = pltpu.make_async_copy(streams, stage, lsem.at[0])
    stage_copy.start()

    def cols(i):
        return pl.ds(pl.multiple_of(i * MAIN, MAIN), MAIN)

    own = [
        pltpu.make_async_copy(
            streams.at[s, :, pl.ds(0, MAIN)], xbuf.at[pl.ds(s * TOK, TOK), cols(x)], lsem.at[1 + s]
        )
        for s in range(2)
    ]
    for c in own:
        c.start()
    wcopies = []
    for p, w in enumerate((wk, wq, wv)):
        for i in range(NX):
            wcopies.append(
                pltpu.make_async_copy(
                    w.at[pl.ds(i * DW, MAIN), :], raw.at[p, pl.ds(i * MAIN, MAIN), :], wsem.at[p, i]
                )
            )
            wcopies.append(
                pltpu.make_async_copy(
                    w.at[pl.ds(i * DW + MAIN, TAIL), :],
                    raw.at[p, pl.ds(NX * MAIN + i * 64, TAIL), :],
                    wsem.at[p, NX + i],
                )
            )
    for c in wcopies:
        c.start()

    pl.semaphore_wait(barrier, len(partners))

    def main_copy(d, c):
        s, t = c // (NC // 2), (c % (NC // 2)) * CH
        return rcopy(
            streams.at[s, pl.ds(t, CH), pl.ds(0, MAIN)],
            xbuf.at[pl.ds(c * CH, CH), cols(x)],
            xs.at[d, c], xr.at[d, c], {"head": side[d]},
        )

    def main_fwd(d, c):
        half = xbuf.at[pl.ds(c * CH + d * (CH // 2), CH // 2), cols(side[1 - d])]
        return rcopy(half, half, fs.at[d, c], fr.at[d, c], {"head": side[d]})

    def tail_copy(d, s):
        part = tbuf.at[x, pl.ds(s * 256, 256), :]
        return rcopy(part, part, ts.at[d, s], tr.at[d, s], {"head": side[d]})

    def tail_fwd(d, s):
        part = tbuf.at[side[1 - d], pl.ds(s * 256 + d * 128, 128), :]
        return rcopy(part, part, us.at[d, s], ur.at[d, s], {"head": side[d]})

    def both(f, c, act):
        for d in range(2):
            getattr(f(d, c), act)()

    both(main_copy, 0, "start")
    stage_copy.wait()
    for s in range(2):
        lo = stage[s, pl.ds(0, 256), pl.ds(MAIN, TAIL)].astype(F32)
        hi = stage[s, pl.ds(256, 256), pl.ds(MAIN, TAIL)].astype(F32)
        gap = jnp.zeros((256, 16), F32)
        tbuf[x, pl.ds(s * 256, 256), :] = jnp.concatenate([lo, gap, hi, gap], axis=1).astype(BF16)
    both(tail_copy, 0, "start")
    both(main_copy, 1, "start")

    for c in wcopies:
        c.wait()
    lane = lax.broadcasted_iota(jnp.int32, (LN, LN), 1)

    def spread(b, _):
        r = pl.ds(pl.multiple_of(b * LN, LN), LN)
        for p in range(3):
            block = raw[p, r, :].astype(F32)
            for h in range(NH):
                piece = jnp.concatenate(
                    [block[:, h * HD : (h + 1) * HD], jnp.zeros((LN, LN - HD), F32)], axis=1
                )
                wcat[r, pl.ds(p * PW + h * LN, LN)] = piece.astype(BF16)
        return _

    lax.fori_loop(0, KW // LN, spread, 0)
    for i in range(NX):
        wcat[pl.ds(NX * MAIN + i * 64 + TAIL, 16), :] = jnp.zeros((16, 3 * PW), BF16)
    for c in own:
        c.wait()

    def tails(s):
        for half in range(2):
            for pair in range(2):
                a = tbuf[2 * pair, pl.ds(s * 256, 256), :].astype(F32)
                b = tbuf[2 * pair + 1, pl.ds(s * 256, 256), :].astype(F32)
                o = 64 * half
                tile = jnp.concatenate([a[:, o : o + 64], b[:, o : o + 64]], axis=1)
                xbuf[pl.ds(s * TOK + half * 256, 256), pl.ds(NX * MAIN + pair * LN, LN)] = tile.astype(BF16)

    def project(c):
        rows = pl.ds(c * CH, CH)

        def piece(first, relu):
            def body(n, _):
                w = pl.ds(pl.multiple_of(n * 256, 256), 256)
                r = jnp.dot(xbuf[rows, :], wcat[:, w], preferred_element_type=F32)
                if relu:
                    r = jnp.maximum(r, 0.0)
                qkv[rows, w] = r.astype(BF16)
                return _

            return body

        lax.fori_loop(0, 5, piece(0, True), 0)
        lax.fori_loop(5, 7, piece(5, False), 0)
        w = pl.ds(7 * 256, LN)
        qkv[rows, w] = jnp.dot(xbuf[rows, :], wcat[:, w], preferred_element_type=F32).astype(BF16)

    def states(s):
        rows = pl.ds(s * TOK, TOK)
        for h in range(NH):
            k = qkv[rows, pl.ds(h * LN, LN)]
            v = qkv[rows, pl.ds(2 * PW + h * LN, LN)]
            r = lax.dot_general(k, v, (((0,), (0,)), ((), ())), preferred_element_type=F32)
            st32[s, pl.ds(h * LN, LN), :] = r
            st16[s, pl.ds(h * LN, LN), :] = r.astype(BF16)

    def quarter(i):
        return pl.ds(pl.multiple_of(i * QR, QR), QR)

    def scatter(s, d):
        to = (y + d) % NY
        return rcopy(
            st16.at[s, quarter(to), :], rsbuf.at[s, d - 1], ys.at[s, d - 1], yr.at[s, d - 1], {"tok": to}
        )

    def collect(s):
        total = st32[s, quarter(y), :]
        for d in range(1, NY):
            scatter(s, d).wait_recv()
            total = total + rsbuf[s, d - 1].astype(F32)
        return total

    def gather(s, d):
        part = tot.at[s, quarter(y), :]
        return rcopy(part, part, ys.at[2 + s, d - 1], yr.at[2 + s, d - 1], {"tok": (y + d) % NY})

    core_copy = rcopy(csend, crecv, cs.at[0], cr.at[0], {"group": mate})
    pre_copy = rcopy(psend, precv, cs.at[1], cr.at[1], {"group": mate})

    def zcopy(d):
        return rcopy(
            zsend, zrecv.at[d - 1], zs.at[d - 1], zr.at[d - 1], {"group": ((z + d) % NZ) * 2 + core}
        )

    def eighth(i):
        return pl.ds(pl.multiple_of(i * ER, ER), ER)

    def read(s):
        for h in range(NH):
            pass
        for t in range(TOK // CH):
            rows = pl.ds(s * TOK + t * CH, CH)
            heads = []
            for h in range(NH):
                q = qkv[rows, pl.ds(PW + h * LN, LN)]
                r = jnp.dot(q, tot[s, pl.ds(h * LN, LN), :], preferred_element_type=F32)
                mean = jnp.sum(r * r, axis=1, keepdims=True) * (1.0 / HD)
                r = r * lax.rsqrt(mean + 1e-06)
                heads.append(r[:, :HD])
            packed = jnp.concatenate(heads, axis=1) * gain[...]
            obuf[s, pl.ds(t * CH, CH), :] = packed.astype(BF16)

    def chain(step):
        if step == 4:
            cst[...] = collect(0)
            csend[...] = cst[...].astype(BF16)
            core_copy.start()
        elif step == 5:
            core_copy.wait_recv()
            zsend[...] = (cst[eighth(core), :] + crecv[eighth(core), :].astype(F32)).astype(BF16)
            for d in range(1, NZ):
                zcopy(d).start()
        elif step == 6:
            acc = jnp.zeros((ER, LN), F32)
            for d in range(1, NZ):
                zcopy(d).wait_recv()
                acc = acc + jnp.where(z >= d, zrecv[d - 1].astype(F32), 0.0)
            pfx[eighth(core), :] = acc
            psend[...] = acc.astype(BF16)
            pre_copy.start()
        elif step == 7:
            pre_copy.wait_recv()
            pfx[eighth(1 - core), :] = precv[...].astype(F32)
            pfx[...] = pfx[...] + jnp.where(core == 1, crecv[...].astype(F32), 0.0)
            tot[0, quarter(y), :] = (pfx[...] + cst[...]).astype(BF16)
            for d in range(1, NY):
                gather(0, d).start()

    half = NC // 2
    for c in range(NC + 1):
        if c < NC:
            both(main_copy, c, "wait_recv")
            both(main_fwd, c, "start")
            if c % half == 0:
                both(tail_copy, c // half, "wait_recv")
                both(tail_fwd, c // half, "start")
            if c + 2 < NC:
                if c + 2 == half:
                    both(tail_copy, 1, "start")
                both(main_copy, c + 2, "start")
        if c >= 1:
            b = c - 1
            if b % half == 0:
                both(tail_fwd, b // half, "wait_recv")
                tails(b // half)
            both(main_fwd, b, "wait_recv")
            project(b)
            if b == half - 1:
                states(0)
                for d in range(1, NY):
                    scatter(0, d).start()
            chain(b)
    states(1)
    for d in range(1, NY):
        scatter(1, d).start()
    for d in range(1, NY):
        gather(0, d).wait_recv()
    read(0)
    out_copies = [pltpu.make_async_copy(obuf.at[s], out.at[s], osem.at[s]) for s in range(2)]
    out_copies[0].start()
    tot[1, quarter(y), :] = (collect(1) + pfx[...]).astype(BF16)
    for d in range(1, NY):
        gather(1, d).start()
    for d in range(1, NY):
        gather(1, d).wait_recv()
    read(1)
    out_copies[1].start()

    for c in range(NC):
        both(main_copy, c, "wait_send")
        both(main_fwd, c, "wait_send")
    for s in range(2):
        both(tail_copy, s, "wait_send")
        both(tail_fwd, s, "wait_send")
        for d in range(1, NY):
            scatter(s, d).wait_send()
            gather(s, d).wait_send()
    core_copy.wait_send()
    pre_copy.wait_send()
    for d in range(1, NZ):
        zcopy(d).wait_send()
    for c in out_copies:
        c.wait()


def local(streams, w_query, w_key, w_value, gain):
    any_spec = pl.BlockSpec(memory_space=pl.ANY)
    vmem = pltpu.VMEM
    dma = pltpu.SemaphoreType.DMA
    return pl.pallas_call(
        kernel,
        out_shape=jax.ShapeDtypeStruct(streams.shape, BF16),
        in_specs=[any_spec] * 4 + [pl.BlockSpec(memory_space=pltpu.VMEM)],
        out_specs=any_spec,
        scratch_shapes=[
            vmem((3, KW, DW), BF16),
            vmem((KW, 3 * PW), BF16),
            vmem((2, TOK, DW), BF16),
            vmem((ROWS, KW), BF16),
            vmem((NX, TOK, LN), BF16),
            vmem((ROWS, 3 * PW), BF16),
            vmem((2, TOK, DW), BF16),
            vmem((2, PW, LN), F32),
            vmem((2, PW, LN), BF16),
            vmem((2, NY - 1, QR, LN), BF16),
            vmem((QR, LN), F32),
            vmem((QR, LN), BF16),
            vmem((QR, LN), BF16),
            vmem((ER, LN), BF16),
            vmem((NZ - 1, ER, LN), BF16),
            vmem((ER, LN), BF16),
            vmem((ER, LN), BF16),
            vmem((QR, LN), F32),
            vmem((2, PW, LN), BF16),
            dma((3,)),
            dma((3, 2 * NX)),
            dma((2,)),
            dma((2, NC)), dma((2, NC)),
            dma((2, NC)), dma((2, NC)),
            dma((2, 2)), dma((2, 2)),
            dma((2, 2)), dma((2, 2)),
            dma((4, NY - 1)), dma((4, NY - 1)),
            dma((2,)), dma((2,)),
            dma((NZ - 1,)), dma((NZ - 1,)),
        ],
        compiler_params=pltpu.CompilerParams(
            collective_id=0, has_side_effects=True, vmem_limit_bytes=60 * 1024 * 1024
        ),
        name="linear_attention",
    )(streams, w_query, w_key, w_value, gain.reshape(1, DW))


def solution(mesh):
    return jax.shard_map(
        local,
        mesh=mesh,
        in_specs=(
            P(None, ("group", "tok"), "head"),
            P(None, "head"),
            P(None, "head"),
            P(None, "head"),
            P("head"),
        ),
        out_specs=P(None, ("group", "tok"), "head"),
        check_vma=False,
    )
```
